32 devices in a mesh: blk: 8 (over z, core), grp: 4 (over y, x).
Axes of the slice: x: 2, y: 2, z: 4, core: 2. Of those that a mesh axis runs over, the one named last changes fastest.
Arguments:
- state: float32 [4, 5, 128, 256], P('grp', None, 'blk'), may hold values from -6 to 6
- advection: float32 [4, 2, 128, 256], P('grp', None, 'blk'), may hold values from 0.2 to 1
- viscosity: float32 [4, 2, 128, 256], P('grp', None, 'blk'), may hold values from 0.01 to 0.2
- donor_cell: int32 [8, 4, 4, 32], P('blk', 'grp'), may hold values from 0 to 3839
- donor_frac: float32 [8, 4, 2, 4, 32], P('blk', 'grp'), may hold values from 0 to 1
- fringe_cell: int32 [8, 4, 4, 32], P('blk', 'grp'), may hold values from 768 to 3327, as said below
- fringe_count: int32 [8, 4, 4], P('blk', 'grp'), may hold values from 1 to 32, as said below
Outputs:
- final_state: float32 [4, 5, 128, 256], P('grp', None, 'blk')
The draws below stay inside these ranges and needn't reach their ends.
Inputs may be any that keep to these rules, and one draw needn't show every extreme that they name: `fringe_cell`: for each receiving block, all entries over source groups and slots are distinct, and every one lies in rows 3 to 12 of the block. `fringe_count`: for every receiving block, one source group has exactly 32 live slots.
All inputs are finite; a program needn't handle non-finite values.
Results may differ from the reference program's by a relative error of at most 0.00005.
Values sent between devices are 32-bit elements; how exact they have to be, the bound alone decides.
A program may use at most 64 MiB of HBM per device.

```python
import math
import jax
import jax.numpy as jnp
from jax import lax

CX = 16
CY = 256
NS = 32
STEPS = 2
BLOCKS = 8
GROUPS = 4
NX = 128


def draw_fringe_cell(key, part):
    interior = (CX - 6) * CY
    keys = jax.random.split(jax.random.fold_in(key, 11), BLOCKS * GROUPS)

    def single(block_key):
        return jax.random.permutation(block_key, interior)[:GROUPS * NS]
    cells = jax.vmap(single)(keys) + 3 * CY
    return cells.reshape(BLOCKS, GROUPS, GROUPS, NS).astype(jnp.int32)


def draw_fringe_count(key, part):
    base = jax.random.randint(jax.random.fold_in(key, 21), (BLOCKS, GROUPS, GROUPS), 1, NS + 1)
    full = jax.random.randint(jax.random.fold_in(key, 22), (BLOCKS, GROUPS), 0, GROUPS)
    marked = jnp.arange(GROUPS, dtype=jnp.int32)[None, None, :] == full[:, :, None]
    return jnp.where(marked, NS, base).astype(jnp.int32)


def touch_ends(drawn, rng, least, high):
    shape = drawn.shape
    index_at = [jax.random.randint(jax.random.fold_in(rng, axis), (), 0, shape[axis]) for axis in range(len(shape))]
    drawn = drawn.at[tuple(index_at)].set(least)
    longest = shape.index(max(shape))
    index_at[longest] = (index_at[longest] + 1) % shape[longest]
    return drawn.at[tuple(index_at)].set(high)


def level_of(rng, shape, pieces, least, largest):
    loudness = 1.0
    for dim, shards_of in pieces:
        draws = jax.random.uniform(jax.random.fold_in(jax.random.fold_in(rng, 6), dim), (shards_of,), jnp.float32, least / len(pieces), largest / len(pieces))
        loudness = loudness * jnp.repeat(jnp.exp(draws), shape[dim] // shards_of).reshape((-1,) + (1,) * (len(shape) - 1 - dim))
    return loudness


def bell_draw(rng, dims, width, limit, pieces=(), kind=jnp.bfloat16):
    values = width * jax.random.normal(rng, dims, jnp.float32)
    if pieces:
        values = values * level_of(rng, dims, pieces, -0.22, 0.18)
    return jnp.clip(values, -limit, limit).astype(kind)


def setup_inputs(seed: int = 0) -> dict:
    streams_of = jax.random.split(jax.random.key(seed), 8)
    return {
        "state": bell_draw(streams_of[0], (GROUPS, 5, NX, CY), 1.0, 6.0, ((0, 4), (2, 8)), jnp.float32),
        "advection": jnp.clip(jnp.exp(math.log(1.0) - 1.609438 * jax.random.uniform(streams_of[1], (GROUPS, 2, NX, CY), jnp.float32) ** level_of(streams_of[1], (GROUPS, 2, NX, CY), ((0, 4), (2, 8)), -0.2, 0.2)), 0.2, 1.0),
        "viscosity": jnp.clip(jnp.exp(math.log(0.2) - 2.9957323 * jax.random.uniform(streams_of[2], (GROUPS, 2, NX, CY), jnp.float32) ** level_of(streams_of[2], (GROUPS, 2, NX, CY), ((0, 4), (2, 8)), -0.2, 0.2)), 0.01, 0.2),
        "donor_cell": touch_ends(jax.random.randint(streams_of[3], (BLOCKS, GROUPS, GROUPS, NS), 0, (CX - 1) * CY), jax.random.fold_in(streams_of[3], 1), 0, ((CX - 1) * CY) - 1).astype(jnp.int32),
        "donor_frac": jnp.clip(1.0 * jax.random.uniform(streams_of[4], (BLOCKS, GROUPS, 2, GROUPS, NS), jnp.float32) ** level_of(streams_of[4], (BLOCKS, GROUPS, 2, GROUPS, NS), ((0, 8), (1, 4)), -0.2, 0.2), 0.0, 1.0),
        "fringe_cell": draw_fringe_cell(jax.random.fold_in(streams_of[7], 71), 0),
        "fringe_count": draw_fringe_count(jax.random.fold_in(streams_of[7], 71), 0),
    }


TIME_STEP = 0.3
SECTION_COEFS = ((0.0, 1.0), (0.75, 0.25), (1.0 / 3.0, 2.0 / 3.0))


def tendency(padded, speed_x, speed_y, visc_x, visc_y):
    rows_n = padded.shape[-2] - 6
    row_axis = padded.ndim - 2

    def along_x(offset):
        return lax.slice_in_dim(padded, 3 + offset, 3 + offset + rows_n, axis=row_axis)

    centre = along_x(0)

    def along_y(offset):
        return jnp.roll(centre, -offset, axis=-1)

    upwind_x = (-2.0 * along_x(-3) + 15.0 * along_x(-2) - 60.0 * along_x(-1) + 20.0 * centre + 30.0 * along_x(1) - 3.0 * along_x(2)) / 60.0
    upwind_y = (-2.0 * along_y(-3) + 15.0 * along_y(-2) - 60.0 * along_y(-1) + 20.0 * centre + 30.0 * along_y(1) - 3.0 * along_y(2)) / 60.0
    central_x = (along_x(-2) - 8.0 * along_x(-1) + 8.0 * along_x(1) - along_x(2)) / 12.0
    central_y = (along_y(-2) - 8.0 * along_y(-1) + 8.0 * along_y(1) - along_y(2)) / 12.0
    second_x = along_x(1) - 2.0 * centre + along_x(-1)
    second_y = along_y(1) - 2.0 * centre + along_y(-1)
    transport = -(speed_x * upwind_x + speed_y * upwind_y) + visc_x * second_x + visc_y * second_y
    diverge = central_x[..., 1, :, :] + central_y[..., 2, :, :]
    grad_x = central_x[..., 4, :, :]
    grad_y = central_y[..., 4, :, :]
    acoustic = jnp.stack([-diverge, -grad_x, -grad_y, jnp.zeros_like(diverge), -diverge], axis=-3)
    return transport + acoustic


def fringe_fill(field, donor_cell, donor_frac, fringe_cell, fringe_count):
    cells = CX * CY
    blocks = field.reshape(GROUPS, 5, BLOCKS, cells).transpose(2, 0, 1, 3)
    corner = donor_cell
    next_col = (corner // CY) * CY + (corner % CY + 1) % CY

    def pick(index):
        flat_index = index.reshape(BLOCKS, GROUPS, 1, GROUPS * NS)
        flat_index = jnp.broadcast_to(flat_index, (BLOCKS, GROUPS, 5, GROUPS * NS))
        return jnp.take_along_axis(blocks, flat_index, axis=3).reshape(BLOCKS, GROUPS, 5, GROUPS, NS)

    frac_x = donor_frac[:, :, 0][:, :, None]
    frac_y = donor_frac[:, :, 1][:, :, None]
    values = (1.0 - frac_x) * (1.0 - frac_y) * pick(corner) + frac_x * (1.0 - frac_y) * pick(corner + CY)
    values = values + (1.0 - frac_x) * frac_y * pick(next_col) + frac_x * frac_y * pick(next_col + CY)
    received = values.transpose(0, 3, 2, 1, 4).reshape(BLOCKS, GROUPS, 5, GROUPS * NS)
    live = jnp.arange(NS, dtype=jnp.int32)[None, None, None, :] < fringe_count[..., None]
    target = jnp.where(live, fringe_cell, cells).reshape(BLOCKS, GROUPS, GROUPS * NS)

    def place(block, index, value):
        return block.at[:, index].set(value, mode="drop")

    filled = jax.vmap(jax.vmap(place))(blocks, target, received)
    return filled.transpose(1, 2, 0, 3).reshape(GROUPS, 5, NX, CY)


def reference(state, advection, viscosity, donor_cell, donor_frac, fringe_cell, fringe_count):
    speed_x = advection[:, 0:1]
    speed_y = advection[:, 1:2]
    visc_x = viscosity[:, 0:1]
    visc_y = viscosity[:, 1:2]
    start = state
    for step_index in range(STEPS):
        section_field = start
        for weight_old, weight_new in SECTION_COEFS:
            filled = fringe_fill(section_field, donor_cell, donor_frac, fringe_cell, fringe_count)
            padded = jnp.pad(filled, ((0, 0), (0, 0), (3, 3), (0, 0)))
            result = filled + TIME_STEP * tendency(padded, speed_x, speed_y, visc_x, visc_y)
            section_field = weight_old * start + weight_new * result
        start = section_field
    return start
```

```python
import functools

import jax
import jax.numpy as jnp
from jax import lax
from jax.experimental import pallas as pl
from jax.experimental.pallas import tpu as pltpu
from jax.sharding import PartitionSpec as P

STEPS = 2
TIME_STEP = 0.3
SECTION_COEFS = ((0.0, 1.0), (0.75, 0.25), (1.0 / 3.0, 2.0 / 3.0))
UPWIND = {-3: -2.0, -2: 15.0, -1: -60.0, 0: 20.0, 1: 30.0, 2: -3.0}
SECOND = {-1: 1.0, 0: -2.0, 1: 1.0}
OFFSETS = (-3, -2, -1, 1, 2)
LANES = 128
SUB = 8
MESH = pl.DeviceIdType.MESH


def split_bf16(x):
    hi = x.astype(jnp.bfloat16)
    lo = (x - hi.astype(jnp.float32)).astype(jnp.bfloat16)
    return hi, lo


def kernel(
    state_hbm,
    adv_hbm,
    visc_hbm,
    cell_hbm,
    frac_hbm,
    fringe_hbm,
    count_ref,
    out_hbm,
    sbuf,
    start_buf,
    pad,
    adv,
    visc,
    cells,
    fracs,
    fringes,
    wide,
    coef,
    pick_mat,
    pick_w,
    place_mat,
    place_rows,
    hit,
    val,
    recv,
    local_sem,
    face_send,
    face_recv,
    slot_send,
    slot_recv,
):
    nvar, rows, halves = sbuf.shape[2], sbuf.shape[3], sbuf.shape[1]
    cols = halves * LANES
    groups, slots = cells.shape
    total = groups * slots
    tiles = total // LANES
    per_tile = LANES // slots
    blk = lax.axis_index("blk")
    grp = lax.axis_index("grp")
    nblk = lax.axis_size("blk")
    has_up = blk > 0
    has_down = blk < nblk - 1
    row_tiles = rows // SUB

    copies = []

    def fetch(src, dst):
        copy = pltpu.make_async_copy(src, dst, local_sem.at[len(copies)])
        copy.start()
        copies.append(copy)
        return copy

    state_copies = [
        fetch(state_hbm.at[0, :, :, pl.ds(h * LANES, LANES)], sbuf.at[0, h]) for h in range(halves)
    ]
    donor_copies = [fetch(cell_hbm.at[0, 0], cells), fetch(frac_hbm.at[0, 0], fracs)]
    fringe_copies = [fetch(fringe_hbm.at[0, 0], fringes)]
    coef_copies = [fetch(adv_hbm.at[0], adv), fetch(visc_hbm.at[0], visc)]

    zero_face = jnp.zeros((halves, nvar, SUB, LANES), jnp.float32)
    for slot in range(2):
        pad[slot, :, :, 0:SUB, :] = zero_face
        pad[slot, :, :, SUB + rows : 2 * SUB + rows, :] = zero_face

    barrier = pltpu.get_barrier_semaphore()
    for j in range(1, groups):
        pl.semaphore_signal(
            barrier, inc=1, device_id=(blk, lax.rem(grp + j, groups)), device_id_type=MESH
        )

    @pl.when(has_up)
    def _():
        pl.semaphore_signal(barrier, inc=1, device_id=(blk - 1, grp), device_id_type=MESH)

    @pl.when(has_down)
    def _():
        pl.semaphore_signal(barrier, inc=1, device_id=(blk + 1, grp), device_id_type=MESH)

    wide[...] = jnp.zeros_like(wide)
    for copy in donor_copies:
        copy.wait()

    lane_block = lax.broadcasted_iota(jnp.int32, (groups, LANES), 1) // slots
    row_id = lax.broadcasted_iota(jnp.int32, (groups, LANES), 0)

    def to_lanes(index, value, sign):
        wide[index, :, 0:slots] = value
        full = wide[index]
        spread = full
        for b in range(1, per_tile):
            spread = jnp.where(lane_block == b, pltpu.roll(full, slots * b, 1), spread)
        pieces = []
        for t in range(tiles):
            source = lax.rem(grp + sign * (t * per_tile + lane_block) + groups, groups)
            pieces.append(
                jnp.sum(jnp.where(row_id == source, spread, 0.0), axis=0, keepdims=True)
            )
        return pieces[0] if tiles == 1 else jnp.concatenate(pieces, axis=1)

    def row_and_col(cell):
        if cols & (cols - 1) == 0:
            return lax.shift_right_logical(cell, cols.bit_length() - 1), cell & (cols - 1)
        return cell // cols, cell % cols

    corner = to_lanes(0, cells[...].astype(jnp.float32), 1).astype(jnp.int32)
    frac_x = to_lanes(1, fracs[0], 1)
    frac_y = to_lanes(2, fracs[1], 1)
    corner_row, corner_col = row_and_col(corner)
    next_col = jnp.where(corner_col == cols - 1, 0, corner_col + 1)
    col_iota = lax.broadcasted_iota(jnp.int32, (cols, total), 0)
    row_iota = lax.broadcasted_iota(jnp.int32, (rows, total), 0)

    def one_hot(iota, index):
        return jnp.where(iota == index, 1.0, 0.0)

    pick_mat[:, 0:total] = one_hot(col_iota, corner_col).astype(jnp.bfloat16)
    pick_mat[:, total : 2 * total] = one_hot(col_iota, next_col).astype(jnp.bfloat16)
    row_weight = (1.0 - frac_x) * one_hot(row_iota, corner_row) + frac_x * one_hot(
        row_iota, corner_row + 1
    )
    pick_w[0] = (1.0 - frac_y) * row_weight
    pick_w[1] = frac_y * row_weight

    for copy in state_copies:
        copy.wait()
    for h in range(halves):
        start_buf[h] = sbuf[0, h]

    pl.semaphore_wait(barrier, groups - 1 + has_up.astype(jnp.int32) + has_down.astype(jnp.int32))

    def face_copy(slot, way):
        first = 0 if way == 0 else rows - SUB
        landing = SUB + rows if way == 0 else 0
        return pltpu.make_async_remote_copy(
            src_ref=sbuf.at[slot, :, :, pl.ds(first, SUB), :],
            dst_ref=pad.at[slot, :, :, pl.ds(landing, SUB), :],
            send_sem=face_send.at[slot, way],
            recv_sem=face_recv.at[slot, way],
            device_id=((blk - 1) if way == 0 else (blk + 1), grp),
            device_id_type=MESH,
        )

    def slot_copy(slot, j):
        return pltpu.make_async_remote_copy(
            src_ref=val.at[slot, :, pl.ds((j // per_tile) * LANES, LANES)],
            dst_ref=recv.at[slot, j],
            send_sem=slot_send.at[slot, j],
            recv_sem=slot_recv.at[slot, j],
            device_id=(blk, lax.rem(grp + j, groups)),
            device_id_type=MESH,
        )

    def send_faces(slot):
        @pl.when(has_up)
        def _():
            face_copy(slot, 0).start()

        @pl.when(has_down)
        def _():
            face_copy(slot, 1).start()

    def send_slots(slot):
        s = [sbuf[slot, h].reshape(nvar * rows, LANES) for h in range(halves)]
        whole = s[0] if halves == 1 else jnp.concatenate(s, axis=1)
        hi, lo = split_bf16(whole)
        mat = pick_mat[...]
        got = jnp.dot(hi, mat, preferred_element_type=jnp.float32) + jnp.dot(
            lo, mat, preferred_element_type=jnp.float32
        )
        here = got[:, 0:total].reshape(nvar, rows, total)
        there = got[:, total : 2 * total].reshape(nvar, rows, total)
        val[slot] = jnp.sum(here * pick_w[0][None] + there * pick_w[1][None], axis=1)
        for j in range(groups - 1, 0, -1):
            slot_copy(slot, j).start()

    def prepare():
        for copy in fringe_copies:
            copy.wait()
        target = to_lanes(3, fringes[...].astype(jnp.float32), -1).astype(jnp.int32)
        lane_id = lax.broadcasted_iota(jnp.int32, (1, total), 1)
        lane_slot = lax.rem(lane_id, slots)
        live = jnp.zeros((1, total), jnp.int32)
        for j in range(groups):
            source = lax.rem(grp - j + groups, groups)
            live = jnp.where(lane_id // slots == j, count_ref[0, 0, source], live)
        target_row, target_col = row_and_col(target)
        target_rows = jnp.where((row_iota == target_row) & (lane_slot < live), 1.0, 0.0)
        place_rows[...] = target_rows
        target_cols = one_hot(col_iota, target_col)
        by_slot = jnp.transpose(target_cols).astype(jnp.bfloat16)
        place_mat[0:total, :] = by_slot
        place_mat[total : 2 * total, :] = by_slot
        hit[...] = jnp.dot(
            target_rows.astype(jnp.bfloat16), by_slot, preferred_element_type=jnp.float32
        )
        for copy in coef_copies:
            copy.wait()
        for h in range(halves):
            window = slice(h * LANES, (h + 1) * LANES)
            centre = 1.0
            for d in range(2):
                speed = adv[d, :, window] * (-TIME_STEP / 60.0)
                visco = visc[d, :, window] * TIME_STEP
                for n, o in enumerate(OFFSETS):
                    c = speed * UPWIND[o]
                    if o in SECOND:
                        c = c + visco * SECOND[o]
                    coef[d * len(OFFSETS) + n, h] = c
                centre = centre + speed * UPWIND[0] + visco * SECOND[0]
            coef[2 * len(OFFSETS), h] = centre

    def receive_slots(slot):
        lane = lax.broadcasted_iota(jnp.int32, (nvar, LANES), 1) // slots
        pieces = []
        for t in range(tiles):
            piece = val[slot, :, t * LANES : (t + 1) * LANES]
            for b in range(per_tile):
                j = t * per_tile + b
                if j > 0:
                    slot_copy(slot, j).wait_recv()
                    piece = jnp.where(lane == b, recv[slot, j], piece)
            pieces.append(piece)
        return pieces[0] if tiles == 1 else jnp.concatenate(pieces, axis=1)

    def fill(slot):
        incoming = receive_slots(slot)
        spread = (incoming[:, None, :] * place_rows[...][None]).reshape(nvar * rows, total)
        hi, lo = split_bf16(spread)
        placed = jnp.dot(
            jnp.concatenate([hi, lo], axis=1), place_mat[...], preferred_element_type=jnp.float32
        )
        for h in range(halves):
            window = slice(h * LANES, (h + 1) * LANES)
            hit_h = hit[:, window] > 0.5
            for f in range(nvar):
                pad[slot, h, f, SUB : SUB + rows, :] = jnp.where(
                    hit_h, placed[f * rows : (f + 1) * rows, window], sbuf[slot, h, f]
                )

    lane = lax.broadcasted_iota(jnp.int32, (SUB, LANES), 1)

    def along_y(centre, o):
        rolled = [pltpu.roll(c, (-o) % LANES, 1) for c in centre]
        if o > 0:
            mask = lane < LANES - o
            return [
                jnp.where(mask, rolled[h], rolled[(h + 1) % halves]) for h in range(halves)
            ]
        mask = lane >= -o
        return [jnp.where(mask, rolled[h], rolled[(h - 1) % halves]) for h in range(halves)]

    def advance(slot, old, new, store):
        count = len(OFFSETS)
        for i in range(row_tiles):
            base = SUB + i * SUB
            grads = {}
            results = {}
            for f in range(nvar):
                centre = [pad[slot, h, f, base : base + SUB, :] for h in range(halves)]
                total_f = [
                    coef[2 * count, h, i * SUB : (i + 1) * SUB, :] * centre[h]
                    for h in range(halves)
                ]
                xs, ys = {}, {}
                for n, o in enumerate(OFFSETS):
                    xs[o] = [
                        pad[slot, h, f, base + o : base + o + SUB, :] for h in range(halves)
                    ]
                    ys[o] = along_y(centre, o)
                    for h in range(halves):
                        rows_i = slice(i * SUB, (i + 1) * SUB)
                        total_f[h] = (
                            total_f[h]
                            + coef[n, h, rows_i, :] * xs[o][h]
                            + coef[count + n, h, rows_i, :] * ys[o][h]
                        )

                def central(vals):
                    return [
                        (vals[-2][h] - vals[2][h]) + 8.0 * (vals[1][h] - vals[-1][h])
                        for h in range(halves)
                    ]

                if f in (1, 4):
                    grads[f, 0] = central(xs)
                if f in (2, 4):
                    grads[f, 1] = central(ys)
                results[f] = total_f
            for h in range(halves):
                scale = TIME_STEP / 12.0
                diverge = (grads[1, 0][h] + grads[2, 1][h]) * scale
                results[0][h] = results[0][h] - diverge
                results[4][h] = results[4][h] - diverge
                results[1][h] = results[1][h] - grads[4, 0][h] * scale
                results[2][h] = results[2][h] - grads[4, 1][h] * scale
                for f in range(nvar):
                    rows_i = slice(i * SUB, (i + 1) * SUB)
                    value = results[f][h]
                    if new != 1.0:
                        value = new * value
                    if old != 0.0:
                        value = value + old * start_buf[h, f, rows_i, :]
                    store(h, f, rows_i, value)

    sections = [c for _ in range(STEPS) for c in SECTION_COEFS]
    for n, (old, new) in enumerate(sections):
        slot = n % 2
        last = n == len(sections) - 1
        step_end = (n + 1) % len(SECTION_COEFS) == 0
        send_faces(slot)
        send_slots(slot)
        if n == 0:
            prepare()
        fill(slot)

        @pl.when(has_up)
        def _():
            face_copy(slot, 1).wait_recv()

        @pl.when(has_down)
        def _():
            face_copy(slot, 0).wait_recv()

        def store(h, f, rows_i, value):
            sbuf[1 - slot, h, f, rows_i, :] = value

        advance(slot, old, new, store)
        if step_end and not last:
            for h in range(halves):
                start_buf[h] = sbuf[1 - slot, h]

        @pl.when(has_up)
        def _():
            face_copy(slot, 0).wait_send()

        @pl.when(has_down)
        def _():
            face_copy(slot, 1).wait_send()

        for j in range(1, groups):
            slot_copy(slot, j).wait_send()

    final = len(sections) % 2
    writes = [
        pltpu.make_async_copy(
            sbuf.at[final, h], out_hbm.at[0, :, :, pl.ds(h * LANES, LANES)], local_sem.at[h]
        )
        for h in range(halves)
    ]
    for copy in writes:
        copy.start()
    for copy in writes:
        copy.wait()


def body(state, advection, viscosity, donor_cell, donor_frac, fringe_cell, fringe_count):
    _, nvar, rows, cols = state.shape
    groups, slots = donor_cell.shape[2:]
    total = groups * slots
    halves = cols // LANES
    f32 = jnp.float32
    hbm = pl.BlockSpec(memory_space=pl.ANY)
    return pl.pallas_call(
        kernel,
        out_shape=jax.ShapeDtypeStruct(state.shape, f32),
        in_specs=[hbm] * 6 + [pl.BlockSpec(memory_space=pltpu.SMEM)],
        out_specs=hbm,
        scratch_shapes=[
            pltpu.VMEM((2, halves, nvar, rows, LANES), f32),
            pltpu.VMEM((halves, nvar, rows, LANES), f32),
            pltpu.VMEM((2, halves, nvar, rows + 2 * SUB, LANES), f32),
            pltpu.VMEM((2, rows, cols), f32),
            pltpu.VMEM((2, rows, cols), f32),
            pltpu.VMEM((groups, slots), jnp.int32),
            pltpu.VMEM((2, groups, slots), f32),
            pltpu.VMEM((groups, slots), jnp.int32),
            pltpu.VMEM((4, groups, LANES), f32),
            pltpu.VMEM((2 * len(OFFSETS) + 1, halves, rows, LANES), f32),
            pltpu.VMEM((cols, 2 * total), jnp.bfloat16),
            pltpu.VMEM((2, rows, total), f32),
            pltpu.VMEM((2 * total, cols), jnp.bfloat16),
            pltpu.VMEM((rows, total), f32),
            pltpu.VMEM((rows, cols), f32),
            pltpu.VMEM((2, nvar, total), f32),
            pltpu.VMEM((2, groups, nvar, LANES), f32),
            pltpu.SemaphoreType.DMA((halves + 5,)),
            pltpu.SemaphoreType.DMA((2, 2)),
            pltpu.SemaphoreType.DMA((2, 2)),
            pltpu.SemaphoreType.DMA((2, groups)),
            pltpu.SemaphoreType.DMA((2, groups)),
        ],
        compiler_params=pltpu.CompilerParams(collective_id=0, has_side_effects=True),
        name="overset_steps",
    )(state, advection, viscosity, donor_cell, donor_frac, fringe_cell, fringe_count)


def solution(mesh):
    placed = (
        P("grp", None, "blk", None),
        P("grp", None, "blk", None),
        P("grp", None, "blk", None),
        P("blk", "grp", None, None),
        P("blk", "grp", None, None, None),
        P("blk", "grp", None, None),
        P("blk", "grp", None),
    )
    return jax.shard_map(
        body, mesh=mesh, in_specs=placed, out_specs=P("grp", None, "blk", None), check_vma=False
    )
```

```python
import functools

import jax
import jax.numpy as jnp
from jax import lax
from jax.experimental import pallas as pl
from jax.experimental.pallas import tpu as pltpu
from jax.sharding import PartitionSpec as P

STEPS = 2
TIME_STEP = 0.3
SECTION_COEFS = ((0.0, 1.0), (0.75, 0.25), (1.0 / 3.0, 2.0 / 3.0))
UPWIND = {-3: -2.0, -2: 15.0, -1: -60.0, 0: 20.0, 1: 30.0, 2: -3.0}
SECOND = {-1: 1.0, 0: -2.0, 1: 1.0}
OFFSETS = (-3, -2, -1, 1, 2)
LANES = 128
SUB = 8
FACE = 3
MESH = pl.DeviceIdType.MESH


def split_bf16(x):
    hi = x.astype(jnp.bfloat16)
    lo = (x - hi.astype(jnp.float32)).astype(jnp.bfloat16)
    return hi, lo


def kernel(
    state_hbm,
    adv_hbm,
    visc_hbm,
    cell_hbm,
    frac_hbm,
    fringe_hbm,
    count_hbm,
    out_ref,
    sbuf,
    start_buf,
    pad,
    adv,
    visc,
    cells,
    fracs,
    fringes,
    count_ref,
    wide,
    coef,
    pick_mat,
    pick_w,
    place_mat,
    place_rows,
    hit,
    val,
    recv,
    local_sem,
    face_send,
    face_recv,
    slot_send,
    slot_recv,
):
    nvar, rows, halves = sbuf.shape[2], sbuf.shape[3], sbuf.shape[1]
    cols = halves * LANES
    groups, slots = cells.shape
    total = groups * slots
    tiles = total // LANES
    per_tile = LANES // slots
    blk = lax.axis_index("blk")
    grp = lax.axis_index("grp")
    nblk = lax.axis_size("blk")
    has_up = blk > 0
    has_down = blk < nblk - 1
    row_tiles = rows // SUB

    paired = groups & (groups - 1) == 0

    def partner(j):
        return grp ^ j if paired else lax.rem(grp + j, groups)

    def giver(j):
        return grp ^ j if paired else lax.rem(grp - j + groups, groups)

    zero_face = jnp.zeros((halves, nvar, SUB, LANES), jnp.float32)
    for slot in range(2):
        pad[slot, :, :, 0:SUB, :] = zero_face
        pad[slot, :, :, SUB + rows : 2 * SUB + rows, :] = zero_face

    barrier = pltpu.get_barrier_semaphore()
    for j in range(1, groups):
        pl.semaphore_signal(
            barrier, inc=1, device_id=(blk, partner(j)), device_id_type=MESH
        )

    @pl.when(has_up)
    def _():
        pl.semaphore_signal(barrier, inc=1, device_id=(blk - 1, grp), device_id_type=MESH)

    @pl.when(has_down)
    def _():
        pl.semaphore_signal(barrier, inc=1, device_id=(blk + 1, grp), device_id_type=MESH)

    copies = []

    def fetch(src, dst):
        copy = pltpu.make_async_copy(src, dst, local_sem.at[len(copies)])
        copy.start()
        copies.append(copy)
        return copy

    state_copies = [
        fetch(state_hbm.at[0, :, :, pl.ds(h * LANES, LANES)], sbuf.at[0, h]) for h in range(halves)
    ]
    donor_copies = [fetch(cell_hbm.at[0, 0], cells), fetch(frac_hbm.at[0, 0], fracs)]
    fringe_copies = [fetch(fringe_hbm.at[0, 0], fringes), fetch(count_hbm, count_ref)]
    coef_copies = [fetch(adv_hbm.at[0], adv), fetch(visc_hbm.at[0], visc)]

    wide[...] = jnp.zeros_like(wide)
    for copy in donor_copies:
        copy.wait()

    lane_block = lax.broadcasted_iota(jnp.int32, (groups, LANES), 1) // slots
    row_id = lax.broadcasted_iota(jnp.int32, (groups, LANES), 0)

    def to_lanes(index, value, group_of):
        wide[index, :, 0:slots] = value
        full = wide[index]
        spread = full
        for b in range(1, per_tile):
            spread = jnp.where(lane_block == b, pltpu.roll(full, slots * b, 1), spread)
        pieces = []
        for t in range(tiles):
            source = group_of(t * per_tile + lane_block)
            pieces.append(
                jnp.sum(jnp.where(row_id == source, spread, 0.0), axis=0, keepdims=True)
            )
        return pieces[0] if tiles == 1 else jnp.concatenate(pieces, axis=1)

    def row_and_col(cell):
        if cols & (cols - 1) == 0:
            return lax.shift_right_logical(cell, cols.bit_length() - 1), cell & (cols - 1)
        return cell // cols, cell % cols

    corner = to_lanes(0, cells[...].astype(jnp.float32), partner).astype(jnp.int32)
    frac_x = to_lanes(1, fracs[0], partner)
    frac_y = to_lanes(2, fracs[1], partner)
    corner_row, corner_col = row_and_col(corner)
    next_col = jnp.where(corner_col == cols - 1, 0, corner_col + 1)
    col_iota = lax.broadcasted_iota(jnp.int32, (cols, total), 0)
    row_iota = lax.broadcasted_iota(jnp.int32, (rows, total), 0)

    def one_hot(iota, index):
        return jnp.where(iota == index, 1.0, 0.0)

    pick_mat[:, 0:total] = one_hot(col_iota, corner_col).astype(jnp.bfloat16)
    pick_mat[:, total : 2 * total] = one_hot(col_iota, next_col).astype(jnp.bfloat16)
    row_weight = (1.0 - frac_x) * one_hot(row_iota, corner_row) + frac_x * one_hot(
        row_iota, corner_row + 1
    )
    pick_w[0] = (1.0 - frac_y) * row_weight
    pick_w[1] = frac_y * row_weight

    for copy in state_copies:
        copy.wait()
    for h in range(halves):
        start_buf[h] = sbuf[0, h]

    pl.semaphore_wait(barrier, groups - 1 + has_up.astype(jnp.int32) + has_down.astype(jnp.int32))

    def face_copy(slot, way):
        first = 0 if way == 0 else rows - SUB
        off = 0 if way == 0 else SUB - FACE
        landing = SUB + rows if way == 0 else 0
        return pltpu.make_async_remote_copy(
            src_ref=sbuf.at[slot, :, :, pl.ds(first + off, FACE), :],
            dst_ref=pad.at[slot, :, :, pl.ds(landing + off, FACE), :],
            send_sem=face_send.at[slot, way],
            recv_sem=face_recv.at[slot, way],
            device_id=((blk - 1) if way == 0 else (blk + 1), grp),
            device_id_type=MESH,
        )

    def slot_copy(slot, j):
        return pltpu.make_async_remote_copy(
            src_ref=val.at[slot, :, pl.ds((j // per_tile) * LANES, LANES)],
            dst_ref=recv.at[slot, j],
            send_sem=slot_send.at[slot, j],
            recv_sem=slot_recv.at[slot, j],
            device_id=(blk, partner(j)),
            device_id_type=MESH,
        )

    def send_faces(slot):
        @pl.when(has_up)
        def _():
            face_copy(slot, 0).start()

        @pl.when(has_down)
        def _():
            face_copy(slot, 1).start()

    def send_slots(slot):
        s = [sbuf[slot, h].reshape(nvar * rows, LANES) for h in range(halves)]
        whole = s[0] if halves == 1 else jnp.concatenate(s, axis=1)
        hi, lo = split_bf16(whole)
        mat = pick_mat[...]
        got = jnp.dot(hi, mat, preferred_element_type=jnp.float32) + jnp.dot(
            lo, mat, preferred_element_type=jnp.float32
        )
        here = got[:, 0:total].reshape(nvar, rows, total)
        there = got[:, total : 2 * total].reshape(nvar, rows, total)
        val[slot] = jnp.sum(here * pick_w[0][None] + there * pick_w[1][None], axis=1)
        for j in range(groups - 1, 0, -1):
            slot_copy(slot, j).start()

    def prepare():
        for copy in fringe_copies:
            copy.wait()
        target = to_lanes(3, fringes[...].astype(jnp.float32), giver).astype(jnp.int32)
        lane_id = lax.broadcasted_iota(jnp.int32, (1, total), 1)
        lane_slot = lax.rem(lane_id, slots)
        live = jnp.zeros((1, total), jnp.int32)
        for j in range(groups):
            live = jnp.where(lane_id // slots == j, count_ref[0, 0, giver(j)], live)
        target_row, target_col = row_and_col(target)
        target_rows = jnp.where((row_iota == target_row) & (lane_slot < live), 1.0, 0.0)
        place_rows[...] = target_rows
        target_cols = one_hot(col_iota, target_col)
        by_slot = jnp.transpose(target_cols).astype(jnp.bfloat16)
        place_mat[0:total, :] = by_slot
        place_mat[total : 2 * total, :] = by_slot
        hit[...] = jnp.dot(
            target_rows.astype(jnp.bfloat16), by_slot, preferred_element_type=jnp.float32
        )
        for copy in coef_copies:
            copy.wait()
        for h in range(halves):
            window = slice(h * LANES, (h + 1) * LANES)
            centre = 1.0
            for d in range(2):
                speed = adv[d, :, window] * (-TIME_STEP / 60.0)
                visco = visc[d, :, window] * TIME_STEP
                for n, o in enumerate(OFFSETS):
                    c = speed * UPWIND[o]
                    if o in SECOND:
                        c = c + visco * SECOND[o]
                    coef[d * len(OFFSETS) + n, h] = c
                centre = centre + speed * UPWIND[0] + visco * SECOND[0]
            coef[2 * len(OFFSETS), h] = centre

    def receive_slots(slot):
        lane = lax.broadcasted_iota(jnp.int32, (nvar, LANES), 1) // slots
        pieces = []
        for t in range(tiles):
            piece = val[slot, :, t * LANES : (t + 1) * LANES]
            for b in range(per_tile):
                j = t * per_tile + b
                if j > 0:
                    slot_copy(slot, j).wait_recv()
                    piece = jnp.where(lane == b, recv[slot, j], piece)
            pieces.append(piece)
        return pieces[0] if tiles == 1 else jnp.concatenate(pieces, axis=1)

    def fill(slot):
        incoming = receive_slots(slot)
        spread = (incoming[:, None, :] * place_rows[...][None]).reshape(nvar * rows, total)
        hi, lo = split_bf16(spread)
        placed = jnp.dot(
            jnp.concatenate([hi, lo], axis=1), place_mat[...], preferred_element_type=jnp.float32
        )
        for h in range(halves):
            window = slice(h * LANES, (h + 1) * LANES)
            hit_h = hit[:, window] > 0.5
            for f in range(nvar):
                pad[slot, h, f, SUB : SUB + rows, :] = jnp.where(
                    hit_h, placed[f * rows : (f + 1) * rows, window], sbuf[slot, h, f]
                )

    lane = lax.broadcasted_iota(jnp.int32, (SUB, LANES), 1)

    def along_y(centre, o):
        rolled = [pltpu.roll(c, (-o) % LANES, 1) for c in centre]
        if o > 0:
            mask = lane < LANES - o
            return [
                jnp.where(mask, rolled[h], rolled[(h + 1) % halves]) for h in range(halves)
            ]
        mask = lane >= -o
        return [jnp.where(mask, rolled[h], rolled[(h - 1) % halves]) for h in range(halves)]

    def advance(slot, old, new, store):
        count = len(OFFSETS)
        for i in range(row_tiles):
            base = SUB + i * SUB
            grads = {}
            results = {}
            for f in range(nvar):
                centre = [pad[slot, h, f, base : base + SUB, :] for h in range(halves)]
                total_f = [
                    coef[2 * count, h, i * SUB : (i + 1) * SUB, :] * centre[h]
                    for h in range(halves)
                ]
                xs, ys = {}, {}
                for n, o in enumerate(OFFSETS):
                    xs[o] = [
                        pad[slot, h, f, base + o : base + o + SUB, :] for h in range(halves)
                    ]
                    ys[o] = along_y(centre, o)
                    for h in range(halves):
                        rows_i = slice(i * SUB, (i + 1) * SUB)
                        total_f[h] = (
                            total_f[h]
                            + coef[n, h, rows_i, :] * xs[o][h]
                            + coef[count + n, h, rows_i, :] * ys[o][h]
                        )

                def central(vals):
                    return [
                        (vals[-2][h] - vals[2][h]) + 8.0 * (vals[1][h] - vals[-1][h])
                        for h in range(halves)
                    ]

                if f in (1, 4):
                    grads[f, 0] = central(xs)
                if f in (2, 4):
                    grads[f, 1] = central(ys)
                results[f] = total_f
            for h in range(halves):
                scale = TIME_STEP / 12.0
                diverge = (grads[1, 0][h] + grads[2, 1][h]) * scale
                results[0][h] = results[0][h] - diverge
                results[4][h] = results[4][h] - diverge
                results[1][h] = results[1][h] - grads[4, 0][h] * scale
                results[2][h] = results[2][h] - grads[4, 1][h] * scale
                for f in range(nvar):
                    rows_i = slice(i * SUB, (i + 1) * SUB)
                    value = results[f][h]
                    if new != 1.0:
                        value = new * value
                    if old != 0.0:
                        value = value + old * start_buf[h, f, rows_i, :]
                    store(h, f, rows_i, value)

    sections = [c for _ in range(STEPS) for c in SECTION_COEFS]
    for n, (old, new) in enumerate(sections):
        slot = n % 2
        last = n == len(sections) - 1
        step_end = (n + 1) % len(SECTION_COEFS) == 0
        send_faces(slot)
        send_slots(slot)
        if n == 0:
            prepare()
        fill(slot)

        @pl.when(has_up)
        def _():
            face_copy(slot, 1).wait_recv()

        @pl.when(has_down)
        def _():
            face_copy(slot, 0).wait_recv()

        def store(h, f, rows_i, value):
            if last:
                out_ref[0, f, rows_i, h * LANES : (h + 1) * LANES] = value
            else:
                sbuf[1 - slot, h, f, rows_i, :] = value

        advance(slot, old, new, store)
        if step_end and not last:
            for h in range(halves):
                start_buf[h] = sbuf[1 - slot, h]

        @pl.when(has_up)
        def _():
            face_copy(slot, 0).wait_send()

        @pl.when(has_down)
        def _():
            face_copy(slot, 1).wait_send()

        for j in range(1, groups):
            slot_copy(slot, j).wait_send()


def body(state, advection, viscosity, donor_cell, donor_frac, fringe_cell, fringe_count):
    _, nvar, rows, cols = state.shape
    groups, slots = donor_cell.shape[2:]
    total = groups * slots
    halves = cols // LANES
    f32 = jnp.float32
    hbm = pl.BlockSpec(memory_space=pl.ANY)
    return pl.pallas_call(
        kernel,
        out_shape=pltpu.VMEM(state.shape, f32),
        in_specs=[hbm] * 7,
        out_specs=pl.BlockSpec(memory_space=pltpu.VMEM),
        scratch_shapes=[
            pltpu.VMEM((2, halves, nvar, rows, LANES), f32),
            pltpu.VMEM((halves, nvar, rows, LANES), f32),
            pltpu.VMEM((2, halves, nvar, rows + 2 * SUB, LANES), f32),
            pltpu.VMEM((2, rows, cols), f32),
            pltpu.VMEM((2, rows, cols), f32),
            pltpu.VMEM((groups, slots), jnp.int32),
            pltpu.VMEM((2, groups, slots), f32),
            pltpu.VMEM((groups, slots), jnp.int32),
            pltpu.SMEM(fringe_count.shape, jnp.int32),
            pltpu.VMEM((4, groups, LANES), f32),
            pltpu.VMEM((2 * len(OFFSETS) + 1, halves, rows, LANES), f32),
            pltpu.VMEM((cols, 2 * total), jnp.bfloat16),
            pltpu.VMEM((2, rows, total), f32),
            pltpu.VMEM((2 * total, cols), jnp.bfloat16),
            pltpu.VMEM((rows, total), f32),
            pltpu.VMEM((rows, cols), f32),
            pltpu.VMEM((2, nvar, total), f32),
            pltpu.VMEM((2, groups, nvar, LANES), f32),
            pltpu.SemaphoreType.DMA((halves + 6,)),
            pltpu.SemaphoreType.DMA((2, 2)),
            pltpu.SemaphoreType.DMA((2, 2)),
            pltpu.SemaphoreType.DMA((2, groups)),
            pltpu.SemaphoreType.DMA((2, groups)),
        ],
        compiler_params=pltpu.CompilerParams(collective_id=0, has_side_effects=True),
        name="overset_steps",
    )(state, advection, viscosity, donor_cell, donor_frac, fringe_cell, fringe_count)


def solution(mesh):
    placed = (
        P("grp", None, "blk", None),
        P("grp", None, "blk", None),
        P("grp", None, "blk", None),
        P("blk", "grp", None, None),
        P("blk", "grp", None, None, None),
        P("blk", "grp", None, None),
        P("blk", "grp", None),
    )
    return jax.shard_map(
        body, mesh=mesh, in_specs=placed, out_specs=P("grp", None, "blk", None), check_vma=False
    )
```

```python
import functools

import jax
import jax.numpy as jnp
from jax import lax
from jax.experimental import pallas as pl
from jax.experimental.pallas import tpu as pltpu
from jax.sharding import PartitionSpec as P

STEPS = 2
TIME_STEP = 0.3
SECTION_COEFS = ((0.0, 1.0), (0.75, 0.25), (1.0 / 3.0, 2.0 / 3.0))
UPWIND = {-3: -2.0, -2: 15.0, -1: -60.0, 0: 20.0, 1: 30.0, 2: -3.0}
SECOND = {-1: 1.0, 0: -2.0, 1: 1.0}
OFFSETS = (-3, -2, -1, 1, 2)
LANES = 128
SUB = 8
FACE = 3
MESH = pl.DeviceIdType.MESH


def split_bf16(x):
    hi = x.astype(jnp.bfloat16)
    lo = (x - hi.astype(jnp.float32)).astype(jnp.bfloat16)
    return hi, lo


def kernel(
    state_hbm,
    adv_hbm,
    visc_hbm,
    cell_hbm,
    frac_hbm,
    fringe_hbm,
    count_hbm,
    out_ref,
    sbuf,
    start_buf,
    pad,
    adv,
    visc,
    cells,
    fracs,
    fringes,
    count_ref,
    wide,
    coef,
    pick_mat,
    pick_w,
    place_mat,
    place_rows,
    hit,
    val,
    recv,
    local_sem,
    face_send,
    face_recv,
    slot_send,
    slot_recv,
):
    nvar, rows, halves = sbuf.shape[2], sbuf.shape[3], sbuf.shape[1]
    cols = halves * LANES
    groups, slots = cells.shape
    total = groups * slots
    tiles = total // LANES
    per_tile = LANES // slots
    blk = lax.axis_index("blk")
    grp = lax.axis_index("grp")
    nblk = lax.axis_size("blk")
    has_up = blk > 0
    has_down = blk < nblk - 1
    row_tiles = rows // SUB

    paired = groups & (groups - 1) == 0

    def partner(j):
        return grp ^ j if paired else lax.rem(grp + j, groups)

    def giver(j):
        return grp ^ j if paired else lax.rem(grp - j + groups, groups)

    zero_face = jnp.zeros((halves, nvar, SUB, LANES), jnp.float32)
    for slot in range(2):
        pad[slot, :, :, 0:SUB, :] = zero_face
        pad[slot, :, :, SUB + rows : 2 * SUB + rows, :] = zero_face

    barrier = pltpu.get_barrier_semaphore()
    for j in range(1, groups):
        pl.semaphore_signal(
            barrier, inc=1, device_id=(blk, partner(j)), device_id_type=MESH
        )

    @pl.when(has_up)
    def _():
        pl.semaphore_signal(barrier, inc=1, device_id=(blk - 1, grp), device_id_type=MESH)

    @pl.when(has_down)
    def _():
        pl.semaphore_signal(barrier, inc=1, device_id=(blk + 1, grp), device_id_type=MESH)

    copies = []

    def fetch(src, dst):
        copy = pltpu.make_async_copy(src, dst, local_sem.at[len(copies)])
        copy.start()
        copies.append(copy)
        return copy

    state_copies = [
        fetch(state_hbm.at[0, :, :, pl.ds(h * LANES, LANES)], sbuf.at[0, h]) for h in range(halves)
    ]
    donor_copies = [fetch(cell_hbm.at[0, 0], cells), fetch(frac_hbm.at[0, 0], fracs)]
    fringe_copies = [fetch(fringe_hbm.at[0, 0], fringes), fetch(count_hbm, count_ref)]
    coef_copies = [fetch(adv_hbm.at[0], adv), fetch(visc_hbm.at[0], visc)]

    wide[...] = jnp.zeros_like(wide)
    for copy in donor_copies:
        copy.wait()

    lane_block = lax.broadcasted_iota(jnp.int32, (groups, LANES), 1) // slots
    row_id = lax.broadcasted_iota(jnp.int32, (groups, LANES), 0)

    def to_lanes(index, value, group_of):
        wide[index, :, 0:slots] = value
        full = wide[index]
        spread = full
        for b in range(1, per_tile):
            spread = jnp.where(lane_block == b, pltpu.roll(full, slots * b, 1), spread)
        pieces = []
        for t in range(tiles):
            source = group_of(t * per_tile + lane_block)
            pieces.append(
                jnp.sum(jnp.where(row_id == source, spread, 0.0), axis=0, keepdims=True)
            )
        return pieces[0] if tiles == 1 else jnp.concatenate(pieces, axis=1)

    def row_and_col(cell):
        if cols & (cols - 1) == 0:
            return lax.shift_right_logical(cell, cols.bit_length() - 1), cell & (cols - 1)
        return cell // cols, cell % cols

    corner = to_lanes(0, cells[...].astype(jnp.float32), partner).astype(jnp.int32)
    frac_x = to_lanes(1, fracs[0], partner)
    frac_y = to_lanes(2, fracs[1], partner)
    corner_row, corner_col = row_and_col(corner)
    next_col = jnp.where(corner_col == cols - 1, 0, corner_col + 1)
    col_iota = lax.broadcasted_iota(jnp.int32, (cols, total), 0)
    row_iota = lax.broadcasted_iota(jnp.int32, (rows, total), 0)

    def one_hot(iota, index):
        return jnp.where(iota == index, 1.0, 0.0)

    pick_mat[:, 0:total] = one_hot(col_iota, corner_col).astype(jnp.bfloat16)
    pick_mat[:, total : 2 * total] = one_hot(col_iota, next_col).astype(jnp.bfloat16)
    row_weight = (1.0 - frac_x) * one_hot(row_iota, corner_row) + frac_x * one_hot(
        row_iota, corner_row + 1
    )
    pick_w[0] = (1.0 - frac_y) * row_weight
    pick_w[1] = frac_y * row_weight

    for copy in state_copies:
        copy.wait()
    for h in range(halves):
        start_buf[h] = sbuf[0, h]

    def face_copy(slot, way):
        first = 0 if way == 0 else rows - SUB
        off = 0 if way == 0 else SUB - FACE
        landing = SUB + rows if way == 0 else 0
        return pltpu.make_async_remote_copy(
            src_ref=sbuf.at[slot, :, :, pl.ds(first + off, FACE), :],
            dst_ref=pad.at[slot, :, :, pl.ds(landing + off, FACE), :],
            send_sem=face_send.at[slot, way],
            recv_sem=face_recv.at[slot, way],
            device_id=((blk - 1) if way == 0 else (blk + 1), grp),
            device_id_type=MESH,
        )

    def slot_copy(slot, j):
        return pltpu.make_async_remote_copy(
            src_ref=val.at[slot, :, pl.ds((j // per_tile) * LANES, LANES)],
            dst_ref=recv.at[slot, j],
            send_sem=slot_send.at[slot, j],
            recv_sem=slot_recv.at[slot, j],
            device_id=(blk, partner(j)),
            device_id_type=MESH,
        )

    def send_faces(slot):
        @pl.when(has_up)
        def _():
            face_copy(slot, 0).start()

        @pl.when(has_down)
        def _():
            face_copy(slot, 1).start()

    def interpolate(slot):
        s = [sbuf[slot, h].reshape(nvar * rows, LANES) for h in range(halves)]
        whole = s[0] if halves == 1 else jnp.concatenate(s, axis=1)
        hi, lo = split_bf16(whole)
        mat = pick_mat[...]
        got = jnp.dot(hi, mat, preferred_element_type=jnp.float32) + jnp.dot(
            lo, mat, preferred_element_type=jnp.float32
        )
        here = got[:, 0:total].reshape(nvar, rows, total)
        there = got[:, total : 2 * total].reshape(nvar, rows, total)
        val[slot] = jnp.sum(here * pick_w[0][None] + there * pick_w[1][None], axis=1)

    def send_slots(slot):
        for j in range(groups - 1, 0, -1):
            slot_copy(slot, j).start()

    def prepare():
        for copy in fringe_copies:
            copy.wait()
        target = to_lanes(3, fringes[...].astype(jnp.float32), giver).astype(jnp.int32)
        lane_id = lax.broadcasted_iota(jnp.int32, (1, total), 1)
        lane_slot = lax.rem(lane_id, slots)
        live = jnp.zeros((1, total), jnp.int32)
        for j in range(groups):
            live = jnp.where(lane_id // slots == j, count_ref[0, 0, giver(j)], live)
        target_row, target_col = row_and_col(target)
        target_rows = jnp.where((row_iota == target_row) & (lane_slot < live), 1.0, 0.0)
        place_rows[...] = target_rows
        target_cols = one_hot(col_iota, target_col)
        by_slot = jnp.transpose(target_cols).astype(jnp.bfloat16)
        place_mat[0:total, :] = by_slot
        place_mat[total : 2 * total, :] = by_slot
        hit[...] = jnp.dot(
            target_rows.astype(jnp.bfloat16), by_slot, preferred_element_type=jnp.float32
        )
        for copy in coef_copies:
            copy.wait()
        for h in range(halves):
            window = slice(h * LANES, (h + 1) * LANES)
            centre = 1.0
            for d in range(2):
                speed = adv[d, :, window] * (-TIME_STEP / 60.0)
                visco = visc[d, :, window] * TIME_STEP
                for n, o in enumerate(OFFSETS):
                    c = speed * UPWIND[o]
                    if o in SECOND:
                        c = c + visco * SECOND[o]
                    coef[d * len(OFFSETS) + n, h] = c
                centre = centre + speed * UPWIND[0] + visco * SECOND[0]
            coef[2 * len(OFFSETS), h] = centre

    def receive_slots(slot):
        lane = lax.broadcasted_iota(jnp.int32, (nvar, LANES), 1) // slots
        pieces = []
        for t in range(tiles):
            piece = val[slot, :, t * LANES : (t + 1) * LANES]
            for b in range(per_tile):
                j = t * per_tile + b
                if j > 0:
                    piece = jnp.where(lane == b, recv[slot, j], piece)
            pieces.append(piece)
        return pieces[0] if tiles == 1 else jnp.concatenate(pieces, axis=1)

    def fill(slot):
        incoming = receive_slots(slot)
        spread = (incoming[:, None, :] * place_rows[...][None]).reshape(nvar * rows, total)
        hi, lo = split_bf16(spread)
        placed = jnp.dot(
            jnp.concatenate([hi, lo], axis=1), place_mat[...], preferred_element_type=jnp.float32
        )
        for h in range(halves):
            window = slice(h * LANES, (h + 1) * LANES)
            hit_h = hit[:, window] > 0.5
            for f in range(nvar):
                pad[slot, h, f, SUB : SUB + rows, :] = jnp.where(
                    hit_h, placed[f * rows : (f + 1) * rows, window], sbuf[slot, h, f]
                )

    lane = lax.broadcasted_iota(jnp.int32, (SUB, LANES), 1)

    def along_y(centre, o):
        rolled = [pltpu.roll(c, (-o) % LANES, 1) for c in centre]
        if o > 0:
            mask = lane < LANES - o
            return [
                jnp.where(mask, rolled[h], rolled[(h + 1) % halves]) for h in range(halves)
            ]
        mask = lane >= -o
        return [jnp.where(mask, rolled[h], rolled[(h - 1) % halves]) for h in range(halves)]

    def advance(slot, old, new, store):
        count = len(OFFSETS)
        for i in range(row_tiles):
            base = SUB + i * SUB
            grads = {}
            results = {}
            for f in range(nvar):
                centre = [pad[slot, h, f, base : base + SUB, :] for h in range(halves)]
                total_f = [
                    coef[2 * count, h, i * SUB : (i + 1) * SUB, :] * centre[h]
                    for h in range(halves)
                ]
                xs, ys = {}, {}
                for n, o in enumerate(OFFSETS):
                    xs[o] = [
                        pad[slot, h, f, base + o : base + o + SUB, :] for h in range(halves)
                    ]
                    ys[o] = along_y(centre, o)
                    for h in range(halves):
                        rows_i = slice(i * SUB, (i + 1) * SUB)
                        total_f[h] = (
                            total_f[h]
                            + coef[n, h, rows_i, :] * xs[o][h]
                            + coef[count + n, h, rows_i, :] * ys[o][h]
                        )

                def central(vals):
                    return [
                        (vals[-2][h] - vals[2][h]) + 8.0 * (vals[1][h] - vals[-1][h])
                        for h in range(halves)
                    ]

                if f in (1, 4):
                    grads[f, 0] = central(xs)
                if f in (2, 4):
                    grads[f, 1] = central(ys)
                results[f] = total_f
            for h in range(halves):
                scale = TIME_STEP / 12.0
                diverge = (grads[1, 0][h] + grads[2, 1][h]) * scale
                results[0][h] = results[0][h] - diverge
                results[4][h] = results[4][h] - diverge
                results[1][h] = results[1][h] - grads[4, 0][h] * scale
                results[2][h] = results[2][h] - grads[4, 1][h] * scale
                for f in range(nvar):
                    rows_i = slice(i * SUB, (i + 1) * SUB)
                    value = results[f][h]
                    if new != 1.0:
                        value = new * value
                    if old != 0.0:
                        value = value + old * start_buf[h, f, rows_i, :]
                    store(h, f, rows_i, value)

    sections = [c for _ in range(STEPS) for c in SECTION_COEFS]
    for n, (old, new) in enumerate(sections):
        slot = n % 2
        last = n == len(sections) - 1
        step_end = (n + 1) % len(SECTION_COEFS) == 0
        interpolate(slot)
        if n == 0:
            arrivals = groups - 1 + has_up.astype(jnp.int32) + has_down.astype(jnp.int32)
            pl.semaphore_wait(barrier, arrivals)
        send_slots(slot)
        send_faces(slot)
        if n == 0:
            prepare()

        @pl.when(has_up)
        def _():
            face_copy(slot, 1).wait_recv()
            face_copy(slot, 0).wait_send()

        @pl.when(has_down)
        def _():
            face_copy(slot, 0).wait_recv()
            face_copy(slot, 1).wait_send()

        for j in range(1, groups):
            slot_copy(slot, j).wait_send()
        for j in range(1, groups):
            slot_copy(slot, j).wait_recv()
        fill(slot)

        def store(h, f, rows_i, value):
            if last:
                out_ref[0, f, rows_i, h * LANES : (h + 1) * LANES] = value
            else:
                sbuf[1 - slot, h, f, rows_i, :] = value

        advance(slot, old, new, store)
        if step_end and not last:
            for h in range(halves):
                start_buf[h] = sbuf[1 - slot, h]


def body(state, advection, viscosity, donor_cell, donor_frac, fringe_cell, fringe_count):
    _, nvar, rows, cols = state.shape
    groups, slots = donor_cell.shape[2:]
    total = groups * slots
    halves = cols // LANES
    f32 = jnp.float32
    hbm = pl.BlockSpec(memory_space=pl.ANY)
    return pl.pallas_call(
        kernel,
        out_shape=pltpu.VMEM(state.shape, f32),
        in_specs=[hbm] * 7,
        out_specs=pl.BlockSpec(memory_space=pltpu.VMEM),
        scratch_shapes=[
            pltpu.VMEM((2, halves, nvar, rows, LANES), f32),
            pltpu.VMEM((halves, nvar, rows, LANES), f32),
            pltpu.VMEM((2, halves, nvar, rows + 2 * SUB, LANES), f32),
            pltpu.VMEM((2, rows, cols), f32),
            pltpu.VMEM((2, rows, cols), f32),
            pltpu.VMEM((groups, slots), jnp.int32),
            pltpu.VMEM((2, groups, slots), f32),
            pltpu.VMEM((groups, slots), jnp.int32),
            pltpu.SMEM(fringe_count.shape, jnp.int32),
            pltpu.VMEM((4, groups, LANES), f32),
            pltpu.VMEM((2 * len(OFFSETS) + 1, halves, rows, LANES), f32),
            pltpu.VMEM((cols, 2 * total), jnp.bfloat16),
            pltpu.VMEM((2, rows, total), f32),
            pltpu.VMEM((2 * total, cols), jnp.bfloat16),
            pltpu.VMEM((rows, total), f32),
            pltpu.VMEM((rows, cols), f32),
            pltpu.VMEM((2, nvar, total), f32),
            pltpu.VMEM((2, groups, nvar, LANES), f32),
            pltpu.SemaphoreType.DMA((halves + 6,)),
            pltpu.SemaphoreType.DMA((2, 2)),
            pltpu.SemaphoreType.DMA((2, 2)),
            pltpu.SemaphoreType.DMA((2, groups)),
            pltpu.SemaphoreType.DMA((2, groups)),
        ],
        compiler_params=pltpu.CompilerParams(collective_id=0, has_side_effects=True),
        name="overset_steps",
    )(state, advection, viscosity, donor_cell, donor_frac, fringe_cell, fringe_count)


def solution(mesh):
    placed = (
        P("grp", None, "blk", None),
        P("grp", None, "blk", None),
        P("grp", None, "blk", None),
        P("blk", "grp", None, None),
        P("blk", "grp", None, None, None),
        P("blk", "grp", None, None),
        P("blk", "grp", None),
    )
    return jax.shard_map(
        body, mesh=mesh, in_specs=placed, out_specs=P("grp", None, "blk", None), check_vma=False
    )
```
